32 devices in a mesh: wide: 8 (over z, y), narrow: 4 (over x, core).
Axes of the slice: x: 2, y: 2, z: 4, core: 2. Of those that a mesh axis runs over, the one named last changes fastest.
Arguments:
- spectra: bfloat16 [128, 32, 1024], P(None, 'narrow', 'wide'), may hold values from -6 to 6
- response: bfloat16 [12, 128, 32, 1024], P(None, None, 'narrow', 'wide'), may hold values from -0.5 to 0.5
- observed: bfloat16 [128, 32, 1024], P('wide', 'narrow'), may hold values from -6 to 6
- column_profile: float32 [32, 1024], P('wide'), as said below
- row_kernel: float32 [32, 5], P('wide'), may hold values from 0.1 to 0.4
- noise_weight: float32 [128], P('wide'), may hold values from 0.3 to 3
- cutoff: int32 [32], P('wide'), may hold values from 128 to 512
- owner: int32 [8], replicated, may hold values from 0 to 7, each once
Outputs:
- gradient: float32 [12, 32, 1024], P(None, 'narrow', 'wide')
The draws below stay inside these ranges and needn't reach their ends.
Inputs may be any that keep to these rules, and one draw needn't show every extreme that they name: `owner`: each value 0 .. 7 appears once. `column_profile`: positive.
All inputs are finite; a program needn't handle non-finite values.
Results may differ from the reference program's by a relative error of at most 0.0029.
Values may be sent and summed in bfloat16 or wider, within the bound.
A program may use at most 64 MiB of HBM per device.

```python
import math
import jax
import jax.numpy as jnp
from jax import lax

W = 32
SPEC = 128
P_SIZE = 12
HALF = 2
NT = 8
NC = 1024
NR = 32


def draw_column_profile(key, part):
    first, second = jax.random.split(key)
    column = jnp.arange(NC, dtype=jnp.int32)
    distance = jnp.minimum(column, NC - column).astype(jnp.float32)
    core = jnp.exp(-0.5 * (distance / 1.5) ** 2)
    wings = 2.0 / (jnp.sqrt(NC * 1.0) * (1.0 + distance / (NC / 8.0)))
    rough = jnp.exp(jax.random.uniform(first, (W, NC), jnp.float32, math.log(0.5), math.log(2.0)))
    level = jnp.exp(jax.random.uniform(second, (W, 1), jnp.float32, math.log(0.35), math.log(0.7)))
    return level * (core + wings)[None, :] * rough


def with_ends(result, stream_key, smallest, high):
    index_at = [jax.random.randint(jax.random.fold_in(stream_key, axis), (), 0, length) for axis, length in enumerate(result.shape)]
    longest = result.shape.index(max(result.shape))
    next_to = index_at[:longest] + [(index_at[longest] + 1) % result.shape[longest]] + index_at[longest + 1:]
    return result.at[tuple(index_at)].set(smallest).at[tuple(next_to)].set(high)


def block_scale(rng, dims, pieces, least, top_value):
    def one(dim, parts):
        steps = jax.random.uniform(jax.random.fold_in(jax.random.fold_in(rng, 6), dim), (parts,), jnp.float32, least / len(pieces), top_value / len(pieces))
        return jnp.repeat(jnp.exp(steps), dims[dim] // parts).reshape((-1,) + (1,) * (len(dims) - dim - 1))

    factor_of = one(*pieces[0])
    for cut in pieces[1:]:
        factor_of = factor_of * one(*cut)
    return factor_of


def centred(stream_key, dims, scale, most, cuts=(), kind=jnp.bfloat16):
    entries = jax.random.normal(stream_key, dims, jnp.float32) * scale
    if len(cuts) > 0:
        entries = block_scale(stream_key, dims, cuts, -0.22, 0.18) * entries
    return jnp.clip(entries, min=-most, max=most).astype(kind)


def setup_inputs(seed: int = 0) -> dict:
    streams_of = jax.random.split(jax.random.key(seed), 9)
    return {
        "spectra": centred(streams_of[0], (SPEC, NR, NC), 1.0, 6.0, ((1, 4), (2, 8))),
        "response": centred(streams_of[1], (P_SIZE, SPEC, NR, NC), SPEC ** -0.5, 0.5, ((2, 4), (3, 8))),
        "observed": centred(streams_of[2], (SPEC, NR, NC), 1.0, 6.0, ((0, 8), (1, 4))),
        "column_profile": draw_column_profile(jax.random.fold_in(streams_of[8], 71), 0),
        "row_kernel": jnp.clip(0.1 + 0.3 * jax.random.uniform(streams_of[4], (W, 2 * HALF + 1), jnp.float32) ** block_scale(streams_of[4], (W, 2 * HALF + 1), ((0, 8),), -0.2, 0.2), 0.1, 0.4),
        "noise_weight": jnp.clip(jnp.exp(math.log(3.0) - 2.3025851 * jax.random.uniform(streams_of[5], (SPEC,), jnp.float32) ** block_scale(streams_of[5], (SPEC,), ((0, 8),), -0.2, 0.2)), 0.3, 3.0),
        "cutoff": with_ends(jax.random.randint(streams_of[6], (W,), NC // 8, NC // 2 + 1), jax.random.fold_in(streams_of[6], 1), NC // 8, (NC // 2 + 1) - 1).astype(jnp.int32),
        "owner": jax.random.permutation(streams_of[7], NT).astype(jnp.int32),
    }


def reference(spectra, response, observed, column_profile, row_kernel, noise_weight, cutoff, owner):
    channels, rows, columns = spectra.shape
    count = owner.shape[0]
    tile = columns // count
    tiled = spectra.reshape(W, 4, rows, count, tile)
    ordered = jnp.take(tiled, owner, axis=3).reshape(W, 4, rows, columns)
    freq = jnp.arange(columns, dtype=jnp.int32)
    distance = jnp.minimum(freq, columns - freq)
    keep = (distance[None, :] < cutoff[:, None]).astype(column_profile.dtype)
    transfer = jnp.fft.fft(column_profile, axis=-1) * keep

    def forward(group):
        values, gain = group
        spectrum = jnp.fft.fft(values.astype(jnp.float32), axis=-1) * gain
        return jnp.real(jnp.fft.ifft(spectrum, axis=-1)).astype(jnp.bfloat16)

    image = lax.map(forward, (ordered, transfer))
    padded = jnp.pad(image.astype(jnp.float32), ((0, 0), (0, 0), (HALF, HALF), (0, 0)))
    blurred = jnp.zeros((W, 4, rows, columns), jnp.float32)
    for lag in range(2 * HALF + 1):
        blurred = blurred + row_kernel[:, lag][:, None, None, None] * padded[:, :, lag:lag + rows]
    target = observed.reshape(W, 4, rows, columns).astype(jnp.float32)
    weights = noise_weight.reshape(W, 4)[:, :, None, None]
    misfit = (weights * (blurred - target)).astype(jnp.bfloat16)
    padded = jnp.pad(misfit.astype(jnp.float32), ((0, 0), (0, 0), (HALF, HALF), (0, 0)))
    spread = jnp.zeros((W, 4, rows, columns), jnp.float32)
    for lag in range(2 * HALF + 1):
        offset = 2 * HALF - lag
        spread = spread + row_kernel[:, lag][:, None, None, None] * padded[:, :, offset:offset + rows]
    spread = spread.astype(jnp.bfloat16)
    back = lax.map(forward, (spread, jnp.conj(transfer))).reshape(W, 4, rows, count, tile)
    restored = jnp.zeros_like(back).at[:, :, :, owner, :].set(back).reshape(channels, rows, columns)
    restored_wide = restored.astype(jnp.float32)

    def project(layer):
        return jnp.sum(layer.astype(jnp.float32) * restored_wide, axis=0)

    return lax.map(project, response)
```

```python
import functools
import math

import jax
import jax.numpy as jnp
import numpy as np
from jax import lax
from jax.experimental import pallas as pl
from jax.experimental.pallas import tpu as pltpu
from jax.sharding import PartitionSpec as P


def with_halo(shard, sides, width):
    for axis, dim in sides:
        peers, length = (lax.axis_size(axis), shard.shape[dim])
        up = [(i, (i + 1) % peers) for i in range(peers - 1)]
        down = [(j, i) for i, j in up]
        last = lax.slice_in_dim(shard, length - width, length, axis=dim)
        leading = lax.slice_in_dim(shard, 0, width, axis=dim)
        before = lax.ppermute(last, axis, up)
        after = lax.ppermute(leading, axis, down)
        shard = jnp.concatenate([before, shard, after], axis=dim)
    return shard


def tile_order(values, owner, forward):
    count = owner.shape[0]
    tiles = jnp.arange(count, dtype=jnp.int32)
    select = (owner[None, :] == tiles[:, None]).astype(values.dtype)
    if forward:
        mixed = jnp.einsum("wsrak,at->wsrtk", values, select, preferred_element_type=jnp.float32)
    else:
        mixed = jnp.einsum("wsrtk,at->wsrak", values, select, preferred_element_type=jnp.float32)
    return mixed.astype(values.dtype)


def phase_table(size_in, size_out, period):
    left_index = jnp.arange(size_in, dtype=jnp.int32)[:, None]
    right_index = jnp.arange(size_out, dtype=jnp.int32)[None, :]
    angle = 2.0 * math.pi / period * (left_index * right_index % period).astype(jnp.float32)
    return (jnp.cos(angle), jnp.sin(angle))


def complex_product(form, value_real, value_imag, table_real, table_imag):

    def contract(left_side, right_side):
        return jnp.einsum(form, left_side, right_side, precision=lax.Precision.HIGHEST)

    if value_imag is None:
        return (contract(value_real, table_real), contract(value_real, table_imag))
    first_real = contract(value_real, table_real) - contract(value_imag, table_imag)
    first_imag = contract(value_real, table_imag) + contract(value_imag, table_real)
    return (first_real, first_imag)


def forward_transform(values, count, tile):
    columns = count * tile
    outer_cos, outer_sin = phase_table(count, count, count)
    segment_real, segment_imag = complex_product(
        "...tk,tf->...fk", values, None, outer_cos, -outer_sin
    )
    twist_cos, twist_sin = phase_table(count, tile, columns)
    turned_real = segment_real * twist_cos + segment_imag * twist_sin
    turned_imag = segment_imag * twist_cos - segment_real * twist_sin
    inner_cos, inner_sin = phase_table(tile, tile, tile)
    return complex_product("...fk,kg->...fg", turned_real, turned_imag, inner_cos, -inner_sin)


def inverse_transform(spec_real, spec_imag, count, tile):
    columns = count * tile
    inner_cos, inner_sin = phase_table(tile, tile, tile)
    segment_real, segment_imag = complex_product(
        "...fg,gk->...fk", spec_real, spec_imag, inner_cos, inner_sin
    )
    twist_cos, twist_sin = phase_table(count, tile, columns)
    turned_real = segment_real * twist_cos - segment_imag * twist_sin
    turned_imag = segment_imag * twist_cos + segment_real * twist_sin
    outer_cos, outer_sin = phase_table(count, count, count)
    real_part = jnp.einsum(
        "...fk,ft->...tk", turned_real, outer_cos, precision=lax.Precision.HIGHEST
    )
    real_part = real_part - jnp.einsum(
        "...fk,ft->...tk", turned_imag, outer_sin, precision=lax.Precision.HIGHEST
    )
    return real_part / columns


def band_transfer(column_profile, cutoff, count, tile):
    waves = column_profile.shape[0]
    columns = count * tile
    shaped = column_profile.reshape(waves, count, tile)
    gain_real, gain_imag = forward_transform(shaped, count, tile)
    low_index = jnp.arange(count, dtype=jnp.int32)[:, None]
    high_index = jnp.arange(tile, dtype=jnp.int32)[None, :]
    frequency = low_index + count * high_index
    distance = jnp.minimum(frequency, columns - frequency)
    keep = (distance[None, :, :] < cutoff[:, None, None]).astype(jnp.float32)
    return (gain_real * keep, gain_imag * keep)


def convolve(values, gain_real, gain_imag, adjoint):
    count, tile = (values.shape[-2], values.shape[-1])
    part_real, part_imag = forward_transform(values, count, tile)
    use_real = gain_real[:, None, None]
    use_imag = gain_imag[:, None, None]
    if adjoint:
        use_imag = -use_imag
    product_real = part_real * use_real - part_imag * use_imag
    product_imag = part_real * use_imag + part_imag * use_real
    return inverse_transform(product_real, product_imag, count, tile)


def row_blur(padded, kernel, extent, start_of):
    result = jnp.zeros(padded.shape[:2] + (extent, padded.shape[3]), jnp.float32)
    for lag in range(kernel.shape[1]):
        begin = start_of(lag)
        section = padded[:, :, begin : begin + extent].astype(jnp.float32)
        result = result + kernel[:, lag][:, None, None, None] * section
    return result


def strip_plan(
    spectra, response, observed, column_profile, row_kernel, noise_weight, cutoff, owner
):
    channels, rows, width = spectra.shape
    waves = column_profile.shape[0]
    columns = column_profile.shape[1]
    count = owner.shape[0]
    tile = columns // count
    half = (row_kernel.shape[1] - 1) // 2
    gain_real, gain_imag = band_transfer(column_profile, cutoff, count, tile)
    segmented = spectra.reshape(channels // 4, 4, rows, width)

    def forward(items):
        stokes = items.shape[1]
        tiled = items.reshape(waves, stokes, rows, count, tile)
        ordered = tile_order(tiled, owner, True)
        result = convolve(ordered.astype(jnp.float32), gain_real, gain_imag, False)
        return result.reshape(waves, stokes, rows, columns).astype(jnp.bfloat16)

    image = forward(lax.all_to_all(segmented, "wide", split_axis=0, concat_axis=3, tiled=True))
    target = observed.reshape(waves, 4, rows, columns)
    weights = noise_weight.reshape(waves, 4)[:, :, None, None]
    joined = with_halo(jnp.stack([image, target]), (("narrow", 3),), 2 * half)
    extent = rows + 2 * half
    blurred = row_blur(joined[0], row_kernel, extent, lambda lag: lag)
    observed_rows = joined[1, :, :, half : half + extent].astype(jnp.float32)
    global_rows = lax.axis_index("narrow") * rows - half + jnp.arange(extent, dtype=jnp.int32)
    inside = ((global_rows >= 0) & (global_rows < rows * lax.axis_size("narrow"))).astype(
        jnp.float32
    )
    padded_misfit = (weights * (blurred - observed_rows) * inside[:, None]).astype(jnp.bfloat16)
    spread = row_blur(padded_misfit, row_kernel, rows, lambda lag: 2 * half - lag)
    spread = spread.astype(jnp.bfloat16).reshape(waves, 4, rows, count, tile)
    back = convolve(spread.astype(jnp.float32), gain_real, gain_imag, True).astype(jnp.bfloat16)
    restored = tile_order(back, owner, False).reshape(waves, 4, rows, columns)
    returned = lax.all_to_all(restored, "wide", split_axis=3, concat_axis=0, tiled=True)
    pixels = returned.reshape(channels, rows, width)
    return jnp.einsum("pcrx,crx->prx", response, pixels, preferred_element_type=jnp.float32)


HALVES = 1
MESH = pl.DeviceIdType.MESH
HIGHEST = lax.Precision.HIGHEST


def phase_constants(count, tile):
    columns = count * tile
    inner = 2.0 * np.pi / tile * (np.outer(np.arange(tile), np.arange(tile)) % tile)
    wheel = np.concatenate([np.cos(inner), np.sin(inner)], axis=1)
    low = np.arange(count)[None, :, None]
    place = (np.arange(count)[:, None] * tile + np.arange(tile)[None, :])[:, None, :]
    turn = 2.0 * np.pi / columns * (low * place % columns)
    return (
        wheel.astype(np.float32),
        np.cos(turn).astype(np.float32),
        np.sin(turn).astype(np.float32),
    )


def band_kernel(profile, cut, wheel, turn_cos, turn_sin, count, tile):
    columns = count * tile
    real = jnp.zeros((count, tile), jnp.float32)
    imag = jnp.zeros((count, tile), jnp.float32)
    for t in range(count):
        piece = profile[:, t * tile : (t + 1) * tile]
        real = real + piece * turn_cos[t]
        imag = imag - piece * turn_sin[t]
    mixed = jnp.dot(
        jnp.concatenate([real, imag], axis=0),
        wheel,
        precision=HIGHEST,
        preferred_element_type=jnp.float32,
    )
    real = mixed[:count, :tile] + mixed[count:, tile:]
    imag = mixed[count:, :tile] - mixed[:count, tile:]
    low = lax.broadcasted_iota(jnp.int32, (count, tile), 0)
    high = lax.broadcasted_iota(jnp.int32, (count, tile), 1)
    frequency = low + count * high
    distance = jnp.minimum(frequency, columns - frequency)
    keep = jnp.where(distance < cut, 1.0 / columns, 0.0).astype(jnp.float32)
    mixed = jnp.dot(
        jnp.concatenate([real * keep, imag * keep], axis=0),
        wheel,
        precision=HIGHEST,
        preferred_element_type=jnp.float32,
    )
    real = mixed[:count, :tile] - mixed[count:, tile:]
    imag = mixed[:count, tile:] + mixed[count:, :tile]
    pieces = []
    for t in range(count):
        term = real * turn_cos[t] - imag * turn_sin[t]
        pieces.append(jnp.sum(term, axis=0, keepdims=True))
    return jnp.concatenate(pieces, axis=1)


def split_in_two(values):
    coarse = values.astype(jnp.bfloat16)
    fine = (values - coarse.astype(jnp.float32)).astype(jnp.bfloat16)
    return coarse, fine


def shifted_sum(values, taps, offsets):
    rows = values.shape[0]
    place = lax.broadcasted_iota(jnp.int32, values.shape, 0)
    total = None
    for tap, offset in zip(taps, offsets):
        if offset == 0:
            moved = values
        else:
            moved = pltpu.roll(values, (-offset) % rows, 0)
            if offset > 0:
                moved = jnp.where(place < rows - offset, moved, 0.0)
            else:
                moved = jnp.where(place >= -offset, moved, 0.0)
        term = tap * moved
        total = term if total is None else total + term
    return total


def wave_kernel(
    sizes,
    owner_hbm,
    row_hbm,
    weight_hbm,
    cutoff_hbm,
    profile_hbm,
    wheel_hbm,
    cos_hbm,
    sin_hbm,
    spectra_ref,
    response_ref,
    observed_ref,
    out_ref,
    owner_ref,
    row_ref,
    weight_ref,
    cutoff_ref,
    profile_ref,
    wheel_ref,
    cos_ref,
    sin_ref,
    inbox,
    target,
    table,
    flipped,
    ahead,
    behind,
    data,
    outbox,
    restored,
    resp,
    send_in,
    recv_in,
    send_obs,
    recv_obs,
    send_out,
    recv_out,
    resp_sem,
    small_sem,
    known,
):
    wide, narrow, halves, stokes, rows, tile, count, taps, params = sizes
    half = (taps - 1) // 2
    columns = count * tile
    every = wide * narrow
    my_wide = lax.axis_index("wide")
    my_narrow = lax.axis_index("narrow")
    me = my_wide * narrow + my_narrow

    def wrapped(value, limit):
        return jnp.where(value >= limit, value - limit, value)

    group = 2 if wide % 2 == 0 else 1
    pair = 2 if narrow % 2 == 0 else 1
    planes = wide // group
    crowd = group * narrow
    part = stokes // halves
    my_plane = lax.div(my_wide, group)
    my_seat = lax.rem(my_wide, group)
    my_chip = lax.div(my_narrow, pair)
    my_core = lax.rem(my_narrow, pair)
    chips = narrow // pair

    def members_of(plane, own):
        found = []
        for dg in range(group):
            for dx in range(chips):
                for dc in range(pair):
                    if own and dg == 0 and dx == 0 and dc == 0:
                        continue
                    seat = wrapped(my_seat + dg, group)
                    chip = wrapped(my_chip + dx, chips)
                    core = wrapped(my_core + dc, pair)
                    found.append((plane * group + seat, chip * pair + core))
        return found

    across = lax.rem(my_plane + planes // 2, planes)
    if planes == 4:
        far_first = [across, planes - 1 - my_plane, planes - 1 - across, my_plane]
    else:
        far_first = [lax.rem(my_plane + 1 + i, planes) for i in range(planes)]
    others = far_first[:-1]
    line = pair

    small = [
        pltpu.make_async_copy(source, place, small_sem.at[i])
        for i, (source, place) in enumerate(
            (
                (profile_hbm, profile_ref),
                (cos_hbm, cos_ref),
                (sin_hbm, sin_ref),
                (wheel_hbm, wheel_ref),
                (cutoff_hbm, cutoff_ref),
                (owner_hbm, owner_ref),
                (row_hbm, row_ref),
                (weight_hbm, weight_ref),
            )
        )
    ]
    barrier = pltpu.get_barrier_semaphore()
    neighbours = members_of(my_plane, True)
    for plane in others:
        neighbours = neighbours + members_of(plane, False)[:line]
    for place in neighbours:
        pl.semaphore_signal(barrier, inc=1, device_id=place, device_id_type=MESH)
    for copy in small:
        copy.start()
    for h in range(halves):
        pltpu.make_async_copy(
            spectra_ref.at[pl.ds(me * stokes + h * part, part)],
            inbox.at[h, my_wide, my_narrow],
            recv_in.at[h, my_plane],
        ).start()
        pltpu.make_async_copy(
            observed_ref.at[pl.ds(my_narrow * stokes + h * part, part)],
            target.at[h, my_narrow],
            recv_obs.at[h],
        ).start()
    get_resp = pltpu.make_async_copy(response_ref, resp, resp_sem)
    get_resp.start()

    def send_spectra(h, place):
        peer = place[0] * narrow + place[1]
        pltpu.make_async_remote_copy(
            src_ref=spectra_ref.at[pl.ds(peer * stokes + h * part, part)],
            dst_ref=inbox.at[h, my_wide, my_narrow],
            send_sem=send_in,
            recv_sem=recv_in.at[h, my_plane],
            device_id=place,
            device_id_type=MESH,
        ).start()

    def send_observed(h):
        for step in range(1, narrow):
            peer = wrapped(my_narrow + step, narrow)
            pltpu.make_async_remote_copy(
                src_ref=observed_ref.at[pl.ds(peer * stokes + h * part, part)],
                dst_ref=target.at[h, my_narrow],
                send_sem=send_obs,
                recv_sem=recv_obs.at[h],
                device_id=(my_wide, peer),
                device_id_type=MESH,
            ).start()

    pl.semaphore_wait(barrier, len(neighbours))
    for place in members_of(my_plane, True):
        pl.semaphore_signal(known, inc=1, device_id=place, device_id_type=MESH)
    for plane in others:
        for place in members_of(plane, False)[:line]:
            send_spectra(0, place)
    for place in members_of(my_plane, True):
        send_spectra(0, place)
    pl.semaphore_wait(known, crowd - 1)
    for plane in others:
        for place in members_of(plane, False)[line:]:
            send_spectra(0, place)
    send_observed(0)
    for h in range(1, halves):
        for plane in others:
            for place in members_of(plane, False):
                send_spectra(h, place)
        for place in members_of(my_plane, True):
            send_spectra(h, place)
        send_observed(h)

    for copy in small:
        copy.wait()
    kernel_row = band_kernel(
        profile_ref[pl.ds(my_narrow, 1), :],
        cutoff_ref[my_narrow],
        wheel_ref[...],
        cos_ref,
        sin_ref,
        count,
        tile,
    )

    rolled = pltpu.roll(
        jnp.broadcast_to(kernel_row, (tile, columns)), 0, 1, stride=1, stride_axis=0
    )
    for d in range(count):
        block = rolled[:, d * tile : (d + 1) * tile]
        coarse, fine = split_in_two(block)
        table[0, d] = coarse
        table[1, d] = fine
        coarse, fine = split_in_two(block.T)
        flipped[0, d] = coarse
        flipped[1, d] = fine

    for s in range(count):
        plane, seat = divmod(s, group)
        inner = slice(seat * tile, (seat + 1) * tile)
        place = jnp.int32(0)
        for t in range(count):
            place = jnp.where(owner_ref[t] == s, t, place)
        for b in range(count):
            up = lax.rem(b - place + count, count)
            down = lax.rem(b + count - place, count)
            for fine in range(2):
                ahead[fine, plane, inner, b * tile : (b + 1) * tile] = table[fine, up]
                behind[fine, plane, b * tile : (b + 1) * tile, inner] = flipped[fine, down]

    tap_values = [row_ref[my_narrow, k] for k in range(taps)]
    strips = narrow * rows

    for h in range(halves):
        image = None
        for plane in reversed(far_first):
            box = inbox.at[h, pl.ds(plane * group, group)]
            pltpu.make_async_copy(box, box, recv_in.at[h, plane]).wait()
            ordered = []
            for dg in range(group):
                got = inbox[h, plane * group + dg].astype(jnp.float32)
                ordered.append(
                    jnp.concatenate(
                        [got[n, c] for c in range(part) for n in range(narrow)], axis=0
                    )
                )
            ordered = jnp.concatenate(ordered, axis=1).astype(jnp.bfloat16)
            for fine in range(2):
                term = jnp.dot(ordered, ahead[fine, plane], preferred_element_type=jnp.float32)
                image = term if image is None else image + term
        image = image.astype(jnp.bfloat16).astype(jnp.float32)

        pltpu.make_async_copy(target.at[h], target.at[h], recv_obs.at[h]).wait()

        for c in range(part):
            lines = image[c * strips : (c + 1) * strips]
            blurred = shifted_sum(lines, tap_values, [k - half for k in range(taps)])
            seen = jnp.concatenate(
                [target[h, n, c].astype(jnp.float32) for n in range(narrow)], axis=0
            )
            misfit = weight_ref[my_narrow * stokes + h * part + c] * (blurred - seen)
            misfit = misfit.astype(jnp.bfloat16).astype(jnp.float32)
            spread = shifted_sum(misfit, tap_values, [half - k for k in range(taps)])
            data[c * strips : (c + 1) * strips, :] = spread.astype(jnp.bfloat16)

        values = data[...]
        for i, plane in enumerate(far_first):
            back = jnp.dot(
                values, behind[0, plane], preferred_element_type=jnp.float32
            ) + jnp.dot(values, behind[1, plane], preferred_element_type=jnp.float32)
            for dg in range(group):
                for n in range(narrow):
                    for c in range(part):
                        top = (c * narrow + n) * rows
                        outbox[h, plane * group + dg, n, c] = back[
                            top : top + rows, dg * tile : (dg + 1) * tile
                        ].astype(jnp.bfloat16)
            for place in members_of(plane, i == planes - 1):
                pltpu.make_async_remote_copy(
                    src_ref=outbox.at[h, place[0], place[1]],
                    dst_ref=restored.at[h, me],
                    send_sem=send_out.at[h],
                    recv_sem=recv_out.at[h, my_plane],
                    device_id=place,
                    device_id_type=MESH,
                ).start()
        pltpu.make_async_copy(
            outbox.at[h, my_wide, my_narrow], restored.at[h, me], recv_out.at[h, my_plane]
        ).start()

    get_resp.wait()
    totals = [jnp.zeros((rows, tile), jnp.float32) for _ in range(params)]
    for h in range(halves):
        for plane in reversed(far_first):
            box = restored.at[h, pl.ds(plane * crowd, crowd)]
            pltpu.make_async_copy(box, box, recv_out.at[h, plane]).wait()

            def project(step, totals):
                peer = plane * crowd + step
                for c in range(part):
                    pixel = restored[h, peer, c].astype(jnp.float32)
                    totals = [
                        total + resp[p, peer * stokes + h * part + c].astype(jnp.float32) * pixel
                        for p, total in enumerate(totals)
                    ]
                return totals

            totals = lax.fori_loop(0, crowd, project, totals)
    for p in range(params):
        out_ref[p] = totals[p]

    sent = spectra_ref.at[pl.ds(0, (every - 1) * stokes)]
    pltpu.make_async_copy(sent, sent, send_in).wait()
    sent = observed_ref.at[pl.ds(0, (narrow - 1) * stokes)]
    pltpu.make_async_copy(sent, sent, send_obs).wait()
    for h in range(halves):
        sent = restored.at[h, pl.ds(0, every - 1)]
        pltpu.make_async_copy(sent, sent, send_out.at[h]).wait()


def wave_plan(
    spectra, response, observed, column_profile, row_kernel, noise_weight, cutoff, owner
):
    channels, rows, tile = spectra.shape
    params = response.shape[0]
    waves, columns = column_profile.shape
    count = owner.shape[0]
    wide = lax.axis_size("wide")
    narrow = lax.axis_size("narrow")
    every = wide * narrow
    stokes = channels // every
    taps = row_kernel.shape[1]
    group = 2 if wide % 2 == 0 else 1
    halves = HALVES if stokes % HALVES == 0 else 1
    part = stokes // halves
    sizes = (wide, narrow, halves, stokes, rows, tile, count, taps, params)
    vmem = pl.BlockSpec(memory_space=pltpu.VMEM)
    hbm = pl.BlockSpec(memory_space=pltpu.HBM)
    dma = pltpu.SemaphoreType.DMA
    half_type = jnp.bfloat16
    lines = part * narrow * rows
    tables = phase_constants(count, tile)
    return pl.pallas_call(
        functools.partial(wave_kernel, sizes),
        out_shape=pltpu.VMEM((params, rows, tile), jnp.float32),
        in_specs=[hbm] * 11,
        out_specs=vmem,
        scratch_shapes=[
            pltpu.SMEM(owner.shape, jnp.int32),
            pltpu.SMEM(row_kernel.shape, jnp.float32),
            pltpu.SMEM(noise_weight.shape, jnp.float32),
            pltpu.SMEM(cutoff.shape, jnp.int32),
            pltpu.VMEM(column_profile.shape, jnp.float32),
            *[pltpu.VMEM(table.shape, jnp.float32) for table in tables],
            pltpu.VMEM((halves, wide, narrow, part, rows, tile), half_type),
            pltpu.VMEM((halves, narrow, part, rows, columns), half_type),
            pltpu.VMEM((2, count, tile, tile), half_type),
            pltpu.VMEM((2, count, tile, tile), half_type),
            pltpu.VMEM((2, wide // group, group * tile, columns), half_type),
            pltpu.VMEM((2, wide // group, columns, group * tile), half_type),
            pltpu.VMEM((lines, columns), half_type),
            pltpu.VMEM((halves, wide, narrow, part, rows, tile), half_type),
            pltpu.VMEM((halves, every, part, rows, tile), half_type),
            pltpu.VMEM(response.shape, half_type),
            dma,
            dma((halves, wide // group)),
            dma,
            dma((halves,)),
            dma((halves,)),
            dma((halves, wide // group)),
            dma,
            dma((8,)),
            pltpu.SemaphoreType.REGULAR,
        ],
        compiler_params=pltpu.CompilerParams(
            collective_id=0, has_side_effects=True, vmem_limit_bytes=60 * 1024 * 1024
        ),
    )(
        owner,
        row_kernel,
        noise_weight,
        cutoff,
        column_profile,
        *tables,
        spectra,
        response,
        observed,
    )


def per_device(
    spectra, response, observed, column_profile, row_kernel, noise_weight, cutoff, owner
):
    channels, rows, tile = spectra.shape
    waves, columns = column_profile.shape
    count = owner.shape[0]
    one_each = waves == lax.axis_size("narrow") and count == lax.axis_size("wide")
    plan = wave_plan if one_each and rows == 8 and tile == 128 else strip_plan
    return plan(
        spectra, response, observed, column_profile, row_kernel, noise_weight, cutoff, owner
    )


def solution(mesh):
    return jax.shard_map(
        per_device,
        mesh=mesh,
        in_specs=(
            P(None, "narrow", "wide"),
            P(None, None, "narrow", "wide"),
            P("wide", "narrow", None),
            P("wide", None),
            P("wide", None),
            P("wide"),
            P("wide"),
            P(),
        ),
        out_specs=P(None, "narrow", "wide"),
        check_vma=False,
    )
```

```python
import functools
import math

import jax
import jax.numpy as jnp
import numpy as np
from jax import lax
from jax.experimental import pallas as pl
from jax.experimental.pallas import tpu as pltpu
from jax.sharding import PartitionSpec as P


def with_halo(shard, sides, width):
    for axis, dim in sides:
        peers, length = (lax.axis_size(axis), shard.shape[dim])
        up = [(i, (i + 1) % peers) for i in range(peers - 1)]
        down = [(j, i) for i, j in up]
        last = lax.slice_in_dim(shard, length - width, length, axis=dim)
        leading = lax.slice_in_dim(shard, 0, width, axis=dim)
        before = lax.ppermute(last, axis, up)
        after = lax.ppermute(leading, axis, down)
        shard = jnp.concatenate([before, shard, after], axis=dim)
    return shard


def tile_order(values, owner, forward):
    count = owner.shape[0]
    tiles = jnp.arange(count, dtype=jnp.int32)
    select = (owner[None, :] == tiles[:, None]).astype(values.dtype)
    if forward:
        mixed = jnp.einsum("wsrak,at->wsrtk", values, select, preferred_element_type=jnp.float32)
    else:
        mixed = jnp.einsum("wsrtk,at->wsrak", values, select, preferred_element_type=jnp.float32)
    return mixed.astype(values.dtype)


def phase_table(size_in, size_out, period):
    left_index = jnp.arange(size_in, dtype=jnp.int32)[:, None]
    right_index = jnp.arange(size_out, dtype=jnp.int32)[None, :]
    angle = 2.0 * math.pi / period * (left_index * right_index % period).astype(jnp.float32)
    return (jnp.cos(angle), jnp.sin(angle))


def complex_product(form, value_real, value_imag, table_real, table_imag):

    def contract(left_side, right_side):
        return jnp.einsum(form, left_side, right_side, precision=lax.Precision.HIGHEST)

    if value_imag is None:
        return (contract(value_real, table_real), contract(value_real, table_imag))
    first_real = contract(value_real, table_real) - contract(value_imag, table_imag)
    first_imag = contract(value_real, table_imag) + contract(value_imag, table_real)
    return (first_real, first_imag)


def forward_transform(values, count, tile):
    columns = count * tile
    outer_cos, outer_sin = phase_table(count, count, count)
    segment_real, segment_imag = complex_product(
        "...tk,tf->...fk", values, None, outer_cos, -outer_sin
    )
    twist_cos, twist_sin = phase_table(count, tile, columns)
    turned_real = segment_real * twist_cos + segment_imag * twist_sin
    turned_imag = segment_imag * twist_cos - segment_real * twist_sin
    inner_cos, inner_sin = phase_table(tile, tile, tile)
    return complex_product("...fk,kg->...fg", turned_real, turned_imag, inner_cos, -inner_sin)


def inverse_transform(spec_real, spec_imag, count, tile):
    columns = count * tile
    inner_cos, inner_sin = phase_table(tile, tile, tile)
    segment_real, segment_imag = complex_product(
        "...fg,gk->...fk", spec_real, spec_imag, inner_cos, inner_sin
    )
    twist_cos, twist_sin = phase_table(count, tile, columns)
    turned_real = segment_real * twist_cos - segment_imag * twist_sin
    turned_imag = segment_imag * twist_cos + segment_real * twist_sin
    outer_cos, outer_sin = phase_table(count, count, count)
    real_part = jnp.einsum(
        "...fk,ft->...tk", turned_real, outer_cos, precision=lax.Precision.HIGHEST
    )
    real_part = real_part - jnp.einsum(
        "...fk,ft->...tk", turned_imag, outer_sin, precision=lax.Precision.HIGHEST
    )
    return real_part / columns


def band_transfer(column_profile, cutoff, count, tile):
    waves = column_profile.shape[0]
    columns = count * tile
    shaped = column_profile.reshape(waves, count, tile)
    gain_real, gain_imag = forward_transform(shaped, count, tile)
    low_index = jnp.arange(count, dtype=jnp.int32)[:, None]
    high_index = jnp.arange(tile, dtype=jnp.int32)[None, :]
    frequency = low_index + count * high_index
    distance = jnp.minimum(frequency, columns - frequency)
    keep = (distance[None, :, :] < cutoff[:, None, None]).astype(jnp.float32)
    return (gain_real * keep, gain_imag * keep)


def convolve(values, gain_real, gain_imag, adjoint):
    count, tile = (values.shape[-2], values.shape[-1])
    part_real, part_imag = forward_transform(values, count, tile)
    use_real = gain_real[:, None, None]
    use_imag = gain_imag[:, None, None]
    if adjoint:
        use_imag = -use_imag
    product_real = part_real * use_real - part_imag * use_imag
    product_imag = part_real * use_imag + part_imag * use_real
    return inverse_transform(product_real, product_imag, count, tile)


def row_blur(padded, kernel, extent, start_of):
    result = jnp.zeros(padded.shape[:2] + (extent, padded.shape[3]), jnp.float32)
    for lag in range(kernel.shape[1]):
        begin = start_of(lag)
        section = padded[:, :, begin : begin + extent].astype(jnp.float32)
        result = result + kernel[:, lag][:, None, None, None] * section
    return result


def strip_plan(
    spectra, response, observed, column_profile, row_kernel, noise_weight, cutoff, owner
):
    channels, rows, width = spectra.shape
    waves = column_profile.shape[0]
    columns = column_profile.shape[1]
    count = owner.shape[0]
    tile = columns // count
    half = (row_kernel.shape[1] - 1) // 2
    gain_real, gain_imag = band_transfer(column_profile, cutoff, count, tile)
    segmented = spectra.reshape(channels // 4, 4, rows, width)

    def forward(items):
        stokes = items.shape[1]
        tiled = items.reshape(waves, stokes, rows, count, tile)
        ordered = tile_order(tiled, owner, True)
        result = convolve(ordered.astype(jnp.float32), gain_real, gain_imag, False)
        return result.reshape(waves, stokes, rows, columns).astype(jnp.bfloat16)

    image = forward(lax.all_to_all(segmented, "wide", split_axis=0, concat_axis=3, tiled=True))
    target = observed.reshape(waves, 4, rows, columns)
    weights = noise_weight.reshape(waves, 4)[:, :, None, None]
    joined = with_halo(jnp.stack([image, target]), (("narrow", 3),), 2 * half)
    extent = rows + 2 * half
    blurred = row_blur(joined[0], row_kernel, extent, lambda lag: lag)
    observed_rows = joined[1, :, :, half : half + extent].astype(jnp.float32)
    global_rows = lax.axis_index("narrow") * rows - half + jnp.arange(extent, dtype=jnp.int32)
    inside = ((global_rows >= 0) & (global_rows < rows * lax.axis_size("narrow"))).astype(
        jnp.float32
    )
    padded_misfit = (weights * (blurred - observed_rows) * inside[:, None]).astype(jnp.bfloat16)
    spread = row_blur(padded_misfit, row_kernel, rows, lambda lag: 2 * half - lag)
    spread = spread.astype(jnp.bfloat16).reshape(waves, 4, rows, count, tile)
    back = convolve(spread.astype(jnp.float32), gain_real, gain_imag, True).astype(jnp.bfloat16)
    restored = tile_order(back, owner, False).reshape(waves, 4, rows, columns)
    returned = lax.all_to_all(restored, "wide", split_axis=3, concat_axis=0, tiled=True)
    pixels = returned.reshape(channels, rows, width)
    return jnp.einsum("pcrx,crx->prx", response, pixels, preferred_element_type=jnp.float32)


HALVES = 2
MESH = pl.DeviceIdType.MESH
HIGHEST = lax.Precision.HIGHEST


def phase_constants(count, tile):
    columns = count * tile
    inner = 2.0 * np.pi / tile * (np.outer(np.arange(tile), np.arange(tile)) % tile)
    wheel = np.concatenate([np.cos(inner), np.sin(inner)], axis=1)
    low = np.arange(count)[None, :, None]
    place = (np.arange(count)[:, None] * tile + np.arange(tile)[None, :])[:, None, :]
    turn = 2.0 * np.pi / columns * (low * place % columns)
    return (
        wheel.astype(np.float32),
        np.cos(turn).astype(np.float32),
        np.sin(turn).astype(np.float32),
    )


def band_kernel(profile, cut, wheel, turn_cos, turn_sin, count, tile):
    columns = count * tile
    real = jnp.zeros((count, tile), jnp.float32)
    imag = jnp.zeros((count, tile), jnp.float32)
    for t in range(count):
        piece = profile[:, t * tile : (t + 1) * tile]
        real = real + piece * turn_cos[t]
        imag = imag - piece * turn_sin[t]
    mixed = jnp.dot(
        jnp.concatenate([real, imag], axis=0),
        wheel,
        precision=HIGHEST,
        preferred_element_type=jnp.float32,
    )
    real = mixed[:count, :tile] + mixed[count:, tile:]
    imag = mixed[count:, :tile] - mixed[:count, tile:]
    low = lax.broadcasted_iota(jnp.int32, (count, tile), 0)
    high = lax.broadcasted_iota(jnp.int32, (count, tile), 1)
    frequency = low + count * high
    distance = jnp.minimum(frequency, columns - frequency)
    keep = jnp.where(distance < cut, 1.0 / columns, 0.0).astype(jnp.float32)
    mixed = jnp.dot(
        jnp.concatenate([real * keep, imag * keep], axis=0),
        wheel,
        precision=HIGHEST,
        preferred_element_type=jnp.float32,
    )
    real = mixed[:count, :tile] - mixed[count:, tile:]
    imag = mixed[:count, tile:] + mixed[count:, :tile]
    pieces = []
    for t in range(count):
        term = real * turn_cos[t] - imag * turn_sin[t]
        pieces.append(jnp.sum(term, axis=0, keepdims=True))
    return jnp.concatenate(pieces, axis=1)


def split_in_two(values):
    coarse = values.astype(jnp.bfloat16)
    fine = (values - coarse.astype(jnp.float32)).astype(jnp.bfloat16)
    return coarse, fine


def shifted_sum(values, taps, offsets):
    rows = values.shape[0]
    place = lax.broadcasted_iota(jnp.int32, values.shape, 0)
    total = None
    for tap, offset in zip(taps, offsets):
        if offset == 0:
            moved = values
        else:
            moved = pltpu.roll(values, (-offset) % rows, 0)
            if offset > 0:
                moved = jnp.where(place < rows - offset, moved, 0.0)
            else:
                moved = jnp.where(place >= -offset, moved, 0.0)
        term = tap * moved
        total = term if total is None else total + term
    return total


def wave_kernel(
    sizes,
    owner_hbm,
    row_hbm,
    weight_hbm,
    cutoff_hbm,
    profile_hbm,
    wheel_hbm,
    cos_hbm,
    sin_hbm,
    spectra_ref,
    response_ref,
    observed_ref,
    out_ref,
    owner_ref,
    row_ref,
    weight_ref,
    cutoff_ref,
    profile_ref,
    wheel_ref,
    cos_ref,
    sin_ref,
    inbox,
    target,
    table,
    flipped,
    ahead,
    behind,
    data,
    outbox,
    restored,
    resp,
    send_in,
    recv_in,
    send_obs,
    recv_obs,
    send_out,
    recv_out,
    resp_sem,
    small_sem,
    known,
    stage,
    stage_sem,
):
    wide, narrow, halves, stokes, rows, tile, count, taps, params = sizes
    half = (taps - 1) // 2
    columns = count * tile
    every = wide * narrow
    my_wide = lax.axis_index("wide")
    my_narrow = lax.axis_index("narrow")
    me = my_wide * narrow + my_narrow

    def wrapped(value, limit):
        return jnp.where(value >= limit, value - limit, value)

    group = 2 if wide % 2 == 0 else 1
    pair = 2 if narrow % 2 == 0 else 1
    planes = wide // group
    crowd = group * narrow
    part = stokes // halves
    my_plane = lax.div(my_wide, group)
    my_seat = lax.rem(my_wide, group)
    my_chip = lax.div(my_narrow, pair)
    my_core = lax.rem(my_narrow, pair)
    chips = narrow // pair

    def members_of(plane, own):
        found = []
        for dg in range(group):
            for dx in range(chips):
                for dc in range(pair):
                    if own and dg == 0 and dx == 0 and dc == 0:
                        continue
                    seat = wrapped(my_seat + dg, group)
                    chip = wrapped(my_chip + dx, chips)
                    core = wrapped(my_core + dc, pair)
                    found.append((plane * group + seat, chip * pair + core))
        return found

    across = lax.rem(my_plane + planes // 2, planes)
    if planes == 4:
        far_first = [across, planes - 1 - my_plane, planes - 1 - across, my_plane]
    else:
        far_first = [lax.rem(my_plane + 1 + i, planes) for i in range(planes)]
    others = far_first[:-1]
    if planes == 4:
        odd = lax.rem(my_plane, 2) == 1
        back_first = [
            jnp.where(odd, 0, across),
            jnp.where(odd, planes - my_plane, planes - 1 - my_plane),
            jnp.where(odd, 2, planes - 1 - across),
            my_plane,
        ]
    else:
        back_first = far_first
    line = pair

    small = [
        pltpu.make_async_copy(source, place, small_sem.at[i])
        for i, (source, place) in enumerate(
            (
                (profile_hbm, profile_ref),
                (cos_hbm, cos_ref),
                (sin_hbm, sin_ref),
                (wheel_hbm, wheel_ref),
                (cutoff_hbm, cutoff_ref),
                (owner_hbm, owner_ref),
                (row_hbm, row_ref),
                (weight_hbm, weight_ref),
            )
        )
    ]
    barrier = pltpu.get_barrier_semaphore()
    neighbours = members_of(my_plane, True)
    for plane in others:
        neighbours = neighbours + members_of(plane, False)[:line]
    for place in neighbours:
        pl.semaphore_signal(barrier, inc=1, device_id=place, device_id_type=MESH)
    for copy in small:
        copy.start()
    for h in range(halves):
        pltpu.make_async_copy(
            spectra_ref.at[pl.ds(me * stokes + h * part, part)],
            inbox.at[h, my_wide, my_narrow],
            recv_in.at[h, my_plane],
        ).start()
        pltpu.make_async_copy(
            observed_ref.at[pl.ds(my_narrow * stokes + h * part, part)],
            target.at[h, my_narrow],
            recv_obs.at[h],
        ).start()
    get_stage = pltpu.make_async_copy(spectra_ref, stage, stage_sem)
    get_stage.start()
    get_resp = pltpu.make_async_copy(response_ref, resp, resp_sem)
    get_resp.start()

    def send_spectra(h, place):
        peer = place[0] * narrow + place[1]
        pltpu.make_async_remote_copy(
            src_ref=stage.at[pl.ds(peer * stokes + h * part, part)],
            dst_ref=inbox.at[h, my_wide, my_narrow],
            send_sem=send_in,
            recv_sem=recv_in.at[h, my_plane],
            device_id=place,
            device_id_type=MESH,
        ).start()

    def send_observed(h):
        for step in range(1, narrow):
            peer = wrapped(my_narrow + step, narrow)
            pltpu.make_async_remote_copy(
                src_ref=observed_ref.at[pl.ds(peer * stokes + h * part, part)],
                dst_ref=target.at[h, my_narrow],
                send_sem=send_obs,
                recv_sem=recv_obs.at[h],
                device_id=(my_wide, peer),
                device_id_type=MESH,
            ).start()

    get_stage.wait()
    pl.semaphore_wait(barrier, len(neighbours))
    for place in members_of(my_plane, True):
        pl.semaphore_signal(known, inc=1, device_id=place, device_id_type=MESH)
    for plane in others:
        for place in members_of(plane, False)[:line]:
            send_spectra(0, place)
    for place in members_of(my_plane, True):
        send_spectra(0, place)
    pl.semaphore_wait(known, crowd - 1)
    for plane in others:
        for place in members_of(plane, False)[line:]:
            send_spectra(0, place)
    send_observed(0)
    for h in range(1, halves):
        for plane in others:
            for place in members_of(plane, False):
                send_spectra(h, place)
        for place in members_of(my_plane, True):
            send_spectra(h, place)
        send_observed(h)

    for copy in small:
        copy.wait()
    kernel_row = band_kernel(
        profile_ref[pl.ds(my_narrow, 1), :],
        cutoff_ref[my_narrow],
        wheel_ref[...],
        cos_ref,
        sin_ref,
        count,
        tile,
    )

    rolled = pltpu.roll(
        jnp.broadcast_to(kernel_row, (tile, columns)), 0, 1, stride=1, stride_axis=0
    )
    for d in range(count):
        block = rolled[:, d * tile : (d + 1) * tile]
        coarse, fine = split_in_two(block)
        table[0, d] = coarse
        table[1, d] = fine
        coarse, fine = split_in_two(block.T)
        flipped[0, d] = coarse
        flipped[1, d] = fine

    for s in range(count):
        plane, seat = divmod(s, group)
        inner = slice(seat * tile, (seat + 1) * tile)
        place = jnp.int32(0)
        for t in range(count):
            place = jnp.where(owner_ref[t] == s, t, place)
        for b in range(count):
            up = lax.rem(b - place + count, count)
            down = lax.rem(b + count - place, count)
            for fine in range(2):
                ahead[fine, plane, inner, b * tile : (b + 1) * tile] = table[fine, up]
                behind[fine, plane, b * tile : (b + 1) * tile, inner] = flipped[fine, down]

    tap_values = [row_ref[my_narrow, k] for k in range(taps)]
    strips = narrow * rows

    for h in range(halves):
        image = None
        for plane in reversed(far_first):
            box = inbox.at[h, pl.ds(plane * group, group)]
            pltpu.make_async_copy(box, box, recv_in.at[h, plane]).wait()
            ordered = []
            for dg in range(group):
                got = inbox[h, plane * group + dg].astype(jnp.float32)
                ordered.append(
                    jnp.concatenate(
                        [got[n, c] for c in range(part) for n in range(narrow)], axis=0
                    )
                )
            ordered = jnp.concatenate(ordered, axis=1).astype(jnp.bfloat16)
            for fine in range(2):
                term = jnp.dot(ordered, ahead[fine, plane], preferred_element_type=jnp.float32)
                image = term if image is None else image + term
        image = image.astype(jnp.bfloat16).astype(jnp.float32)

        pltpu.make_async_copy(target.at[h], target.at[h], recv_obs.at[h]).wait()

        for c in range(part):
            lines = image[c * strips : (c + 1) * strips]
            blurred = shifted_sum(lines, tap_values, [k - half for k in range(taps)])
            seen = jnp.concatenate(
                [target[h, n, c].astype(jnp.float32) for n in range(narrow)], axis=0
            )
            misfit = weight_ref[my_narrow * stokes + h * part + c] * (blurred - seen)
            misfit = misfit.astype(jnp.bfloat16).astype(jnp.float32)
            spread = shifted_sum(misfit, tap_values, [half - k for k in range(taps)])
            data[c * strips : (c + 1) * strips, :] = spread.astype(jnp.bfloat16)

        values = data[...]
        for i, plane in enumerate(back_first):
            back = jnp.dot(
                values, behind[0, plane], preferred_element_type=jnp.float32
            ) + jnp.dot(values, behind[1, plane], preferred_element_type=jnp.float32)
            for dg in range(group):
                for n in range(narrow):
                    for c in range(part):
                        top = (c * narrow + n) * rows
                        outbox[h, plane * group + dg, n, c] = back[
                            top : top + rows, dg * tile : (dg + 1) * tile
                        ].astype(jnp.bfloat16)
            if i < planes - 1:
                places = [
                    (plane * group + seat, n) for seat in range(group) for n in range(narrow)
                ]
            else:
                places = members_of(plane, True)
            for place in places:
                pltpu.make_async_remote_copy(
                    src_ref=outbox.at[h, place[0], place[1]],
                    dst_ref=restored.at[h, me],
                    send_sem=send_out.at[h],
                    recv_sem=recv_out.at[h, my_plane],
                    device_id=place,
                    device_id_type=MESH,
                ).start()
        pltpu.make_async_copy(
            outbox.at[h, my_wide, my_narrow], restored.at[h, me], recv_out.at[h, my_plane]
        ).start()

    get_resp.wait()
    totals = [jnp.zeros((rows, tile), jnp.float32) for _ in range(params)]
    for h in range(halves):
        for plane in reversed(far_first):
            box = restored.at[h, pl.ds(plane * crowd, crowd)]
            pltpu.make_async_copy(box, box, recv_out.at[h, plane]).wait()

            def project(step, totals):
                peer = plane * crowd + step
                for c in range(part):
                    pixel = restored[h, peer, c].astype(jnp.float32)
                    totals = [
                        total + resp[p, peer * stokes + h * part + c].astype(jnp.float32) * pixel
                        for p, total in enumerate(totals)
                    ]
                return totals

            totals = lax.fori_loop(0, crowd, project, totals)
    for p in range(params):
        out_ref[p] = totals[p]

    sent = spectra_ref.at[pl.ds(0, (every - 1) * stokes)]
    pltpu.make_async_copy(sent, sent, send_in).wait()
    sent = observed_ref.at[pl.ds(0, (narrow - 1) * stokes)]
    pltpu.make_async_copy(sent, sent, send_obs).wait()
    for h in range(halves):
        sent = restored.at[h, pl.ds(0, every - 1)]
        pltpu.make_async_copy(sent, sent, send_out.at[h]).wait()


def wave_plan(
    spectra, response, observed, column_profile, row_kernel, noise_weight, cutoff, owner
):
    channels, rows, tile = spectra.shape
    params = response.shape[0]
    waves, columns = column_profile.shape
    count = owner.shape[0]
    wide = lax.axis_size("wide")
    narrow = lax.axis_size("narrow")
    every = wide * narrow
    stokes = channels // every
    taps = row_kernel.shape[1]
    group = 2 if wide % 2 == 0 else 1
    halves = HALVES if stokes % HALVES == 0 else 1
    part = stokes // halves
    sizes = (wide, narrow, halves, stokes, rows, tile, count, taps, params)
    vmem = pl.BlockSpec(memory_space=pltpu.VMEM)
    hbm = pl.BlockSpec(memory_space=pltpu.HBM)
    dma = pltpu.SemaphoreType.DMA
    half_type = jnp.bfloat16
    lines = part * narrow * rows
    tables = phase_constants(count, tile)
    return pl.pallas_call(
        functools.partial(wave_kernel, sizes),
        out_shape=pltpu.VMEM((params, rows, tile), jnp.float32),
        in_specs=[hbm] * 11,
        out_specs=vmem,
        scratch_shapes=[
            pltpu.SMEM(owner.shape, jnp.int32),
            pltpu.SMEM(row_kernel.shape, jnp.float32),
            pltpu.SMEM(noise_weight.shape, jnp.float32),
            pltpu.SMEM(cutoff.shape, jnp.int32),
            pltpu.VMEM(column_profile.shape, jnp.float32),
            *[pltpu.VMEM(table.shape, jnp.float32) for table in tables],
            pltpu.VMEM((halves, wide, narrow, part, rows, tile), half_type),
            pltpu.VMEM((halves, narrow, part, rows, columns), half_type),
            pltpu.VMEM((2, count, tile, tile), half_type),
            pltpu.VMEM((2, count, tile, tile), half_type),
            pltpu.VMEM((2, wide // group, group * tile, columns), half_type),
            pltpu.VMEM((2, wide // group, columns, group * tile), half_type),
            pltpu.VMEM((lines, columns), half_type),
            pltpu.VMEM((halves, wide, narrow, part, rows, tile), half_type),
            pltpu.VMEM((halves, every, part, rows, tile), half_type),
            pltpu.VMEM(response.shape, half_type),
            dma,
            dma((halves, wide // group)),
            dma,
            dma((halves,)),
            dma((halves,)),
            dma((halves, wide // group)),
            dma,
            dma((8,)),
            pltpu.SemaphoreType.REGULAR,
            pltpu.VMEM(spectra.shape, half_type),
            dma,
        ],
        compiler_params=pltpu.CompilerParams(
            collective_id=0, has_side_effects=True, vmem_limit_bytes=60 * 1024 * 1024
        ),
    )(
        owner,
        row_kernel,
        noise_weight,
        cutoff,
        column_profile,
        *tables,
        spectra,
        response,
        observed,
    )


def per_device(
    spectra, response, observed, column_profile, row_kernel, noise_weight, cutoff, owner
):
    channels, rows, tile = spectra.shape
    waves, columns = column_profile.shape
    count = owner.shape[0]
    one_each = waves == lax.axis_size("narrow") and count == lax.axis_size("wide")
    plan = wave_plan if one_each and rows == 8 and tile == 128 else strip_plan
    return plan(
        spectra, response, observed, column_profile, row_kernel, noise_weight, cutoff, owner
    )


def solution(mesh):
    return jax.shard_map(
        per_device,
        mesh=mesh,
        in_specs=(
            P(None, "narrow", "wide"),
            P(None, None, "narrow", "wide"),
            P("wide", "narrow", None),
            P("wide", None),
            P("wide", None),
            P("wide"),
            P("wide"),
            P(),
        ),
        out_specs=P(None, "narrow", "wide"),
        check_vma=False,
    )
```
